32 devices in a mesh: lon: 8 (over z, x), lat: 4 (over y, core).
Axes of the slice: x: 2, y: 2, z: 4, core: 2. Of those that a mesh axis runs over, the one named last changes fastest.
Arguments:
- courant: float32 [4, 2, 137, 32, 512], P(None, None, None, 'lon', 'lat'), may hold values from -0.45 to 0.45
- slot_column_cells: int32 [4, 32, 32, 4], P(None, ('lon', 'lat')), may hold values from 0 to 511
- column_counts: int32 [4, 32, 32], P(None, ('lon', 'lat')), may hold values from 1 to 4, as said below
- innovations: float32 [4, 32, 32, 4, 128], P(None, ('lon', 'lat')), may hold values from -6 to 6
- error_weight: float32 [4, 32, 32, 4, 128], P(None, ('lon', 'lat')), may hold values from 0.3 to 3
- weighting: float32 [274, 128], replicated, may hold values from -0.375 to 0.375
Outputs:
- solution: float32 [2, 137, 32, 512], P(None, None, 'lon', 'lat')
- residual: float32 [2, 137, 32, 512], P(None, None, 'lon', 'lat')
The draws below stay inside these ranges and needn't reach their ends.
Inputs may be any that keep to these rules, and one draw needn't show every extreme that they name: `slot_column_cells`: A cell of the sending device's block, numbered longitude-major over its 4 x 128 cells; only slots below the matching count are read. `column_counts`: at every timestep some owner receives 4 live slots from every sending device.
All inputs are finite; a program needn't handle non-finite values.
Results may differ from the reference program's by a relative error of at most 0.00016.
Values sent between devices are 32-bit elements; how exact they have to be, the bound alone decides.
A program may use at most 128 MiB of HBM per device.

```python
import math
import jax
import jax.numpy as jnp
from jax import lax

LEV = 137
CHAN = 128
NT = 4
ITERS = 2
CAP = 4
LONC = 4
LATC = 128
NLON = 32
NLAT = 512
CELLS = 512
N_LAT = 4
DEVICES = 32


def draw_column_counts(key, part):
    level_key = jax.random.fold_in(key, 11)
    count_key = jax.random.fold_in(key, 12)
    owner_key = jax.random.fold_in(key, 13)
    ceiling = jnp.minimum(jnp.power(2, jax.random.randint(level_key, (1, 1, DEVICES), 1, 3)), CAP)
    counts = jax.random.randint(count_key, (NT, DEVICES, DEVICES), ceiling // 2, ceiling + 1)
    crowded = jax.random.randint(owner_key, (NT, 1, 1), 0, DEVICES)
    owner_index = lax.broadcasted_iota(jnp.int32, (NT, DEVICES, DEVICES), 2)
    return jnp.where(owner_index == crowded, CAP, counts).astype(jnp.int32)


def set_ends(values, own_key, low, top_value):
    longest = values.shape.index(max(values.shape))
    spots = []
    for shift in (0, 1):
        where = [jax.random.randint(jax.random.fold_in(own_key, axis), (), 0, length) for axis, length in enumerate(values.shape)]
        where[longest] = (where[longest] + shift) % values.shape[longest]
        spots.append(tuple(where))
    return values.at[spots[0]].set(low).at[spots[1]].set(top_value)


def shard_levels(key, dims, shards, low, high):
    level = 1.0
    for dim, shards_of in shards:
        draws = jax.random.uniform(jax.random.fold_in(jax.random.fold_in(key, 6), dim), (shards_of,), jnp.float32, low / len(shards), high / len(shards))
        level = level * jnp.repeat(jnp.exp(draws), dims[dim] // shards_of).reshape((-1,) + (1,) * (len(dims) - 1 - dim))
    return level


def gaussian(stream_key, dims, deviation, reach, split=(), dtype=jnp.bfloat16):
    factor_of = shard_levels(stream_key, dims, split, -0.22, 0.18) if split else 1.0
    array = jax.random.normal(stream_key, dims, jnp.float32) * deviation * factor_of
    return jnp.minimum(jnp.maximum(array, -reach), reach).astype(dtype)


def setup_inputs(seed: int = 0) -> dict:
    streams_of = jax.random.split(jax.random.key(seed), 7)
    courant = jnp.clip(jax.random.uniform(streams_of[0], (NT, 2, LEV, NLON, NLAT), jnp.float32, -0.45, 0.45) * shard_levels(streams_of[0], (NT, 2, LEV, NLON, NLAT), ((3, 8), (4, 4)), -0.4, 0.0), -0.45, 0.45)
    slot_column_cells = set_ends(jax.random.randint(streams_of[1], (NT, DEVICES, DEVICES, CAP), 0, CELLS), jax.random.fold_in(streams_of[1], 1), 0, CELLS - 1).astype(jnp.int32)
    column_counts = draw_column_counts(jax.random.fold_in(streams_of[6], 71), 0)
    innovations = gaussian(streams_of[3], (NT, DEVICES, DEVICES, CAP, CHAN), 1.0, 6.0, ((1, 32),), jnp.float32)
    error_weight = jnp.clip(jnp.exp(math.log(3.0) - 2.3025851 * jax.random.uniform(streams_of[4], (NT, DEVICES, DEVICES, CAP, CHAN), jnp.float32) ** shard_levels(streams_of[4], (NT, DEVICES, DEVICES, CAP, CHAN), ((1, 32),), -0.2, 0.2)), 0.3, 3.0)
    weighting = gaussian(streams_of[5], (2 * LEV, CHAN), (2 * LEV) ** -0.5, 0.375, (), jnp.float32)
    return {"courant": courant, "slot_column_cells": slot_column_cells, "column_counts": column_counts, "innovations": innovations, "error_weight": error_weight, "weighting": weighting}


def advance(states, east_courant, north_courant):
    from_west = jnp.roll(states, 1, axis=2)
    from_east = jnp.roll(states, -1, axis=2)
    padded = jnp.pad(states, ((0, 0), (0, 0), (0, 0), (1, 1)))
    result = (1.0 - jnp.abs(east_courant) - jnp.abs(north_courant)) * states
    result = result + jnp.maximum(east_courant, 0.0) * from_west
    result = result + jnp.maximum(-east_courant, 0.0) * from_east
    result = result + jnp.maximum(north_courant, 0.0) * padded[:, :, :, :-2]
    result = result + jnp.maximum(-north_courant, 0.0) * padded[:, :, :, 2:]
    return result


def retreat(states, east_courant, north_courant):
    widths = ((0, 0), (0, 0), (0, 0), (1, 1))
    eastward = jnp.maximum(east_courant, 0.0) * states
    westward = jnp.maximum(-east_courant, 0.0) * states
    northward = jnp.pad(jnp.maximum(north_courant, 0.0) * states, widths)
    southward = jnp.pad(jnp.maximum(-north_courant, 0.0) * states, widths)
    result = (1.0 - jnp.abs(east_courant) - jnp.abs(north_courant)) * states
    result = result + jnp.roll(eastward, -1, axis=2)
    result = result + jnp.roll(westward, 1, axis=2)
    result = result + northward[:, :, :, 2:]
    result = result + southward[:, :, :, :-2]
    return result


def reference(courant, slot_column_cells, column_counts, innovations, error_weight, weighting):
    column_depth = 2 * LEV
    cell_total = NLON * NLAT
    highest = lax.Precision.HIGHEST
    sources = lax.broadcasted_iota(jnp.int32, (NT, DEVICES, DEVICES, CAP), 1)
    longitude = (sources // N_LAT) * LONC + slot_column_cells // LATC
    latitude = (sources % N_LAT) * LATC + slot_column_cells % LATC
    flat_index = (longitude * NLAT + latitude).astype(jnp.int32)
    slot_position = lax.broadcasted_iota(jnp.int32, (NT, DEVICES, DEVICES, CAP), 3)
    active = (slot_position < column_counts[:, :, :, None]).astype(jnp.float32)

    def observe(states, time_moment):
        columns = states.reshape(column_depth, cell_total)[:, flat_index[time_moment]]
        columns = columns * active[time_moment]
        return jnp.einsum("kgoc,kh->ogch", columns, weighting, precision=highest)

    def deposit(weighted, time_moment):
        gradient = jnp.einsum("ogch,kh->kgoc", weighted, weighting, precision=highest) * active[time_moment]
        total = jnp.zeros((column_depth, cell_total), jnp.float32)
        total = total.at[:, flat_index[time_moment].reshape(-1)].add(gradient.reshape(column_depth, -1))
        return total.reshape(2, LEV, NLON, NLAT)

    def tangent(states):
        payloads = []
        for time_moment in range(NT):
            states = advance(states, courant[time_moment, 0], courant[time_moment, 1])
            payloads.append(error_weight[time_moment] * observe(states, time_moment))
        return payloads

    def adjoint_sweep(payloads):
        sensitivity = jnp.zeros((2, LEV, NLON, NLAT), jnp.float32)
        for time_moment in reversed(range(NT)):
            sensitivity = sensitivity + deposit(payloads[time_moment], time_moment)
            sensitivity = retreat(sensitivity, courant[time_moment, 0], courant[time_moment, 1])
        return sensitivity

    def hessian(direction):
        return direction + adjoint_sweep(tangent(direction))

    weighted_all = error_weight * innovations
    right_hand_side = adjoint_sweep([weighted_all[time_moment] for time_moment in range(NT)])
    solution = jnp.zeros((2, LEV, NLON, NLAT), jnp.float32)
    residual = right_hand_side
    direction = right_hand_side
    residual_norm = jnp.sum(residual * residual)
    for iteration in range(ITERS):
        hessian_image = hessian(direction)
        step_length = residual_norm / jnp.sum(direction * hessian_image)
        solution = solution + step_length * direction
        residual = residual - step_length * hessian_image
        if iteration + 1 < ITERS:
            updated = jnp.sum(residual * residual)
            direction = residual + (updated / residual_norm) * direction
            residual_norm = updated
    return solution, residual
```

```python
import functools

import jax
import jax.numpy as jnp
from jax import lax
from jax.experimental import pallas as pl
from jax.experimental.pallas import tpu as pltpu
from jax.sharding import PartitionSpec as P

ITERS = 2
CHUNKS = 2
TILE = 24
MESH = pl.DeviceIdType.MESH
F32 = jnp.float32
BF16 = jnp.bfloat16


def split(value):
    high = value.astype(BF16)
    return high, (value - high.astype(F32)).astype(BF16)


def dot(a, b):
    return jnp.dot(a, b, preferred_element_type=F32)


def dot_nt(a, b):
    return lax.dot_general(a, b, (((1,), (1,)), ((), ())), preferred_element_type=F32)


def kernel(
    lon_n, lat_n,
    courant, cells, scale, target, up_w, down_w,
    x_out, r_out,
    p, s, y_acc, v_dep, onehot, up_hi, up_lo, down_hi, down_lo,
    snd, rcv, part1, part2, sums1, sums2,
    ssem, rsem, s1, r1, s2, r2,
):
    times, _, slab, levels, band = courant.shape
    rows_h = 2 * levels // CHUNKS
    per_var = levels // rows_h
    a = lax.axis_index("lon")
    b = lax.axis_index("lat")
    peers = (
        (lax.rem(a + lon_n - 1, lon_n), b),
        (lax.rem(a + 1, lon_n), b),
        (a, lax.rem(b + lat_n - 1, lat_n)),
        (a, lax.rem(b + 1, lat_n)),
    )

    barrier = pltpu.get_barrier_semaphore()
    for off in range(1, lon_n):
        pl.semaphore_signal(barrier, inc=1, device_id=(lax.rem(a + off, lon_n), b), device_id_type=MESH)
    for off in range(1, lat_n):
        pl.semaphore_signal(barrier, inc=1, device_id=(a, lax.rem(b + off, lat_n)), device_id_type=MESH)
    pl.semaphore_wait(barrier, lon_n + lat_n - 2)

    lane = lax.broadcasted_iota(jnp.int32, (TILE, band), 1)
    has_south = (b > 0).astype(F32)
    has_north = (b < lat_n - 1).astype(F32)

    def copies(par, h):
        span = pl.ds(h * rows_h, rows_h)
        return [
            pltpu.make_async_remote_copy(
                src_ref=snd.at[par, d, span],
                dst_ref=rcv.at[par, d, span],
                send_sem=ssem.at[par, h, d],
                recv_sem=rsem.at[par, h, d],
                device_id=peers[d],
                device_id_type=MESH,
            )
            for d in range(4)
        ]

    def start(par, h):
        for copy in copies(par, h):
            copy.start()

    def wait(par, h):
        for copy in copies(par, h):
            copy.wait()

    def tiles(h, body, init=None):
        def step(n, carry):
            at = pl.multiple_of(n * TILE, 8)
            row = pl.ds(pl.multiple_of(h * rows_h + at, 8), TILE)
            crow = pl.ds(pl.multiple_of((h % per_var) * rows_h + at, 8), TILE)
            return body(row, crow, carry)

        return lax.fori_loop(0, rows_h // TILE, step, init)

    def winds(t, crow):
        return (
            [courant[t, 0, i, crow, :] for i in range(slab)],
            [courant[t, 1, i, crow, :] for i in range(slab)],
        )

    def turn(value, shift):
        shift = shift % band
        return value if shift == 0 else pltpu.roll(value, shift, 1)

    def halos(par, row):
        from_south = rcv[par, 3, row, :] * has_south
        from_north = rcv[par, 2, row, :] * has_north
        return rcv[par, 1, row, :], rcv[par, 0, row, :], from_south, from_north

    def shifted(value, halo, i, up):
        if up:
            return jnp.where(lane == 0, turn(halo, -i), turn(value, 1))
        return jnp.where(lane == band - 1, turn(halo, slab - 1 - i), turn(value, -1))

    def advance(t, h, par):
        def body(row, crow, carry):
            u, v = winds(t, crow)
            x = [s[i, row, :] for i in range(slab)]
            west, east, south, north = halos(par, row)
            full = [west] + x + [east]
            for i in range(slab):
                out = (1.0 - jnp.abs(u[i]) - jnp.abs(v[i])) * x[i]
                out += jnp.maximum(u[i], 0.0) * full[i]
                out += jnp.maximum(-u[i], 0.0) * full[i + 2]
                out += jnp.maximum(v[i], 0.0) * shifted(x[i], south, i, True)
                out += jnp.maximum(-v[i], 0.0) * shifted(x[i], north, i, False)
                s[i, row, :] = out
            return carry

        tiles(h, body, 0)

    def retreat(t, h, par):
        def body(row, crow, carry):
            u, v = winds(t, crow)
            y = [s[i, row, :] for i in range(slab)]
            west, east, south, north = halos(par, row)
            plus = [jnp.maximum(u[i], 0.0) * y[i] for i in range(slab)] + [east]
            minus = [west] + [jnp.maximum(-u[i], 0.0) * y[i] for i in range(slab)]
            for i in range(slab):
                out = (1.0 - jnp.abs(u[i]) - jnp.abs(v[i])) * y[i]
                out += plus[i + 1] + minus[i]
                out += shifted(jnp.maximum(v[i], 0.0) * y[i], north, i, False)
                out += shifted(jnp.maximum(-v[i], 0.0) * y[i], south, i, True)
                s[i, row, :] = out
            return carry

        tiles(h, body, 0)

    def put_edges(par, row, west, east, southward, northward):
        snd[par, 0, row, :] = west
        snd[par, 1, row, :] = east
        low = jnp.zeros((TILE, band), F32)
        high = low
        for i in range(slab):
            low = jnp.where(lane == band - slab + i, turn(southward[i], band - slab + i), low)
            high = jnp.where(lane == i, turn(northward[i], i + 1), high)
        snd[par, 2, row, :] = low
        snd[par, 3, row, :] = high

    def send_state(h, par):
        def body(row, crow, carry):
            x = [s[i, row, :] for i in range(slab)]
            put_edges(par, row, x[0], x[-1], x, x)
            return carry

        tiles(h, body, 0)
        start(par, h)

    def send_products(t, h, par):
        def body(row, crow, carry):
            u, v = winds(t, crow)
            y = [s[i, row, :] for i in range(slab)]
            put_edges(
                par, row,
                jnp.maximum(u[0], 0.0) * y[0],
                jnp.maximum(-u[-1], 0.0) * y[-1],
                [jnp.maximum(v[i], 0.0) * y[i] for i in range(slab)],
                [jnp.maximum(-v[i], 0.0) * y[i] for i in range(slab)],
            )
            return carry

        tiles(h, body, 0)
        start(par, h)

    def project(t, h):
        span = pl.ds(h * rows_h, rows_h)
        for i in range(slab):
            high, low = split(s[i, span, :])
            y = dot(up_hi[h], high) + dot(up_hi[h], low) + dot(up_lo[h], high)
            if h == 0:
                y_acc[t, i] = y
            else:
                y_acc[t, i] += y

    def scatter(t, weighted):
        high, low = split(weighted)
        for i in range(slab):
            v_dep[t, i] = dot_nt(high, onehot[t, i]) + dot_nt(low, onehot[t, i])

    def observe(t):
        seen = None
        for i in range(slab):
            high, low = split(y_acc[t, i])
            term = dot(high, onehot[t, i]) + dot(low, onehot[t, i])
            seen = term if seen is None else seen + term
        scatter(t, scale[t] * seen)

    def deposit(t, h, add):
        span = pl.ds(h * rows_h, rows_h)
        for i in range(slab):
            high, low = split(v_dep[t, i])
            d = dot(down_hi[h], high) + dot(down_hi[h], low) + dot(down_lo[h], high)
            if add:
                s[i, span, :] += d
            else:
                s[i, span, :] = d

    def adjoint():
        for h in range(CHUNKS):
            deposit(times - 1, h, False)
            send_products(times - 1, h, 0)

        def step(n, carry):
            t = times - 1 - n
            par = lax.rem(n, 2)
            for h in range(CHUNKS):
                wait(par, h)
                retreat(t, h, par)

                @pl.when(t > 0)
                def _():
                    deposit(t - 1, h, True)
                    send_products(t - 1, h, 1 - par)

            return carry

        lax.fori_loop(0, times, step, 0)

    def tangent():
        def step(t, carry):
            par = lax.rem(t, 2)
            for h in range(CHUNKS):
                wait(par, h)
                advance(t, h, par)

                @pl.when(t < times - 1)
                def _():
                    send_state(h, 1 - par)

                project(t, h)
            observe(t)
            return carry

        lax.fori_loop(0, times, step, 0)

    def across(k, axis, tile, count, me, source, sums, send, receive):
        source[k] = tile
        sums[k, me] = tile
        moves = []
        for off in range(1, count):
            other = lax.rem(me + off, count)
            moves.append(
                pltpu.make_async_remote_copy(
                    src_ref=source.at[k],
                    dst_ref=sums.at[k, me],
                    send_sem=send.at[k, off - 1],
                    recv_sem=receive.at[k, off - 1],
                    device_id=(other, b) if axis == 0 else (a, other),
                    device_id_type=MESH,
                )
            )
        for move in moves:
            move.start()
        for move in moves:
            move.wait()
        total = sums[k, 0]
        for j in range(1, count):
            total = total + sums[k, j]
        return total

    def allsum(k, first, second):
        tile = jnp.concatenate([first, second], axis=0)
        tile = across(k, 0, tile, lon_n, a, part1, sums1, s1, r1)
        tile = across(k, 1, tile, lat_n, b, part2, sums2, s2, r2)
        return jnp.sum(tile[:8], keepdims=True), jnp.sum(tile[8:], keepdims=True)

    def fold(value):
        return value.reshape(TILE // 8, 8, band).sum(0)

    for h in range(CHUNKS):
        up_hi[h], up_lo[h] = split(up_w[h])
        down_hi[h], down_lo[h] = split(down_w[h])
    slots = cells.shape[-1]
    latitude = lax.broadcasted_iota(jnp.int32, (band, slots), 0)
    for t in range(times):
        here = jnp.broadcast_to(cells[t], (band, slots))
        for i in range(slab):
            onehot[t, i] = jnp.where(here == latitude + i * band, 1.0, 0.0).astype(BF16)
        scatter(t, target[t])

    adjoint()
    zero = jnp.zeros((8, band), F32)
    acc = zero
    for h in range(CHUNKS):
        def first(row, crow, acc):
            for i in range(slab):
                value = s[i, row, :]
                p[i, row, :] = value
                r_out[i, row, :] = value
                acc = acc + fold(value * value)
            return acc

        send_state(h, 0)
        acc = tiles(h, first, acc)
    rho, _ = allsum(0, acc, zero)
    for k in range(ITERS):
        last = k + 1 == ITERS
        tangent()
        adjoint()
        pq, qq = zero, zero
        for h in range(CHUNKS):
            def image(row, crow, carry):
                pq, qq = carry
                for i in range(slab):
                    d = p[i, row, :]
                    q = d + s[i, row, :]
                    s[i, row, :] = q
                    pq = pq + fold(d * q)
                    qq = qq + fold(q * q)
                return pq, qq

            pq, qq = tiles(h, image, (pq, qq))
        pq, qq = allsum(1 + k, pq, qq)
        alpha = rho / pq
        if not last:
            rho_new = rho - 2.0 * alpha * pq + alpha * alpha * qq
            beta = rho_new / rho
            rho = rho_new
        for h in range(CHUNKS):
            def update(row, crow, carry):
                for i in range(slab):
                    d = p[i, row, :]
                    if k == 0:
                        x_out[i, row, :] = alpha * d
                    else:
                        x_out[i, row, :] += alpha * d
                    residual = r_out[i, row, :] - alpha * s[i, row, :]
                    r_out[i, row, :] = residual
                    if not last:
                        d = residual + beta * d
                        p[i, row, :] = d
                        s[i, row, :] = d
                return carry

            tiles(h, update, 0)
            if not last:
                send_state(h, 0)


def body(courant, slot_column_cells, column_counts, innovations, error_weight, weighting):
    times, _, levels, slab, band = courant.shape
    owners, cap = slot_column_cells.shape[2:]
    chan = weighting.shape[1]
    slots = owners * cap
    lon_n, lat_n = lax.axis_size("lon"), lax.axis_size("lat")
    deep = -(-levels // 48) * 48
    rows_h = 2 * deep // CHUNKS

    field = jnp.pad(courant.transpose(0, 1, 3, 2, 4), ((0, 0),) * 3 + ((0, deep - levels), (0, 0)))
    weights = jnp.pad(weighting.reshape(2, levels, chan), ((0, 0), (0, deep - levels), (0, 0)))
    down_w = weights.reshape(CHUNKS, rows_h, chan)
    up_w = down_w.transpose(0, 2, 1)
    here = error_weight[:, 0]
    both = jnp.stack([here, here * innovations[:, 0]]).transpose(2, 0, 1, 3, 4)
    both = lax.all_to_all(both, ("lon", "lat"), split_axis=0, concat_axis=0, tiled=True)
    position = lax.broadcasted_iota(jnp.int32, (times, owners, cap), 2)
    live = (position < column_counts[:, 0][:, :, None]).astype(F32).reshape(times, 1, slots)
    both = both.transpose(1, 2, 4, 0, 3).reshape(2, times, chan, slots) * live
    cells = slot_column_cells[:, 0].reshape(times, 1, slots)

    state = (slab, 2 * deep, band)
    vmem = pl.BlockSpec(memory_space=pltpu.VMEM)
    sums = 1 + ITERS
    x, r = pl.pallas_call(
        functools.partial(kernel, lon_n, lat_n),
        out_shape=[jax.ShapeDtypeStruct(state, F32)] * 2,
        in_specs=[vmem] * 6,
        out_specs=[vmem] * 2,
        scratch_shapes=[
            pltpu.VMEM(state, F32),
            pltpu.VMEM(state, F32),
            pltpu.VMEM((times, slab, chan, band), F32),
            pltpu.VMEM((times, slab, chan, band), F32),
            pltpu.VMEM((times, slab, band, slots), BF16),
            pltpu.VMEM((CHUNKS, chan, rows_h), BF16),
            pltpu.VMEM((CHUNKS, chan, rows_h), BF16),
            pltpu.VMEM((CHUNKS, rows_h, chan), BF16),
            pltpu.VMEM((CHUNKS, rows_h, chan), BF16),
            pltpu.VMEM((2, 4, 2 * deep, band), F32),
            pltpu.VMEM((2, 4, 2 * deep, band), F32),
            pltpu.VMEM((sums, 16, band), F32),
            pltpu.VMEM((sums, 16, band), F32),
            pltpu.VMEM((sums, lon_n, 16, band), F32),
            pltpu.VMEM((sums, lat_n, 16, band), F32),
            pltpu.SemaphoreType.DMA((2, CHUNKS, 4)),
            pltpu.SemaphoreType.DMA((2, CHUNKS, 4)),
            pltpu.SemaphoreType.DMA((sums, lon_n - 1)),
            pltpu.SemaphoreType.DMA((sums, lon_n - 1)),
            pltpu.SemaphoreType.DMA((sums, lat_n - 1)),
            pltpu.SemaphoreType.DMA((sums, lat_n - 1)),
        ],
        compiler_params=pltpu.CompilerParams(collective_id=0, has_side_effects=True, vmem_limit_bytes=48 * 2**20),
    )(field, cells, both[0], both[1], up_w, down_w)

    def back(state):
        return state.reshape(slab, 2, deep, band)[:, :, :levels].transpose(1, 2, 0, 3)

    return back(x), back(r)


def solution(mesh):
    owned = ("lon", "lat")
    in_specs = (
        P(None, None, None, "lon", "lat"),
        P(None, owned, None, None),
        P(None, owned, None),
        P(None, owned, None, None, None),
        P(None, owned, None, None, None),
        P(),
    )
    out_specs = (P(None, None, "lon", "lat"), P(None, None, "lon", "lat"))
    return jax.shard_map(body, mesh=mesh, in_specs=in_specs, out_specs=out_specs, check_vma=False)
```

```python
import functools

import jax
import jax.numpy as jnp
from jax import lax
from jax.experimental import pallas as pl
from jax.experimental.pallas import tpu as pltpu
from jax.sharding import PartitionSpec as P

ITERS = 2
CHUNKS = 4
TILE = 24
MESH = pl.DeviceIdType.MESH
F32 = jnp.float32
BF16 = jnp.bfloat16


def split(value):
    high = value.astype(BF16)
    return high, (value - high.astype(F32)).astype(BF16)


def dot(a, b):
    return jnp.dot(a, b, preferred_element_type=F32)


def dot_nt(a, b):
    return lax.dot_general(a, b, (((1,), (1,)), ((), ())), preferred_element_type=F32)


def kernel(
    lon_n, lat_n, valid,
    courant, cells, scale, target, up_w, down_w,
    x_out, r_out,
    p, s, keep, dep, y_acc, v_dep, onehot,
    snd, rcv, part1, part2, sums1, sums2,
    ssem, rsem, s1, r1, s2, r2,
):
    times, _, slab, levels, band = courant.shape
    chan = up_w.shape[1]
    rows_h = 2 * levels // CHUNKS
    per_var = levels // rows_h
    a = lax.axis_index("lon")
    b = lax.axis_index("lat")
    peers = (
        (lax.rem(a + lon_n - 1, lon_n), b),
        (lax.rem(a + 1, lon_n), b),
        (a, lax.rem(b + lat_n - 1, lat_n)),
        (a, lax.rem(b + 1, lat_n)),
    )

    for par in range(2):
        for d in range(4):
            for var in range(2):
                tail = slice(var * levels + valid // 8 * 8, (var + 1) * levels)
                rcv[par, d, tail, :] = jnp.zeros((levels - valid // 8 * 8, band), F32)
    barrier = pltpu.get_barrier_semaphore()
    for off in range(1, lon_n):
        pl.semaphore_signal(barrier, inc=1, device_id=(lax.rem(a + off, lon_n), b), device_id_type=MESH)
    for off in range(1, lat_n):
        pl.semaphore_signal(barrier, inc=1, device_id=(a, lax.rem(b + off, lat_n)), device_id_type=MESH)

    lane = lax.broadcasted_iota(jnp.int32, (TILE, band), 1)
    has_south = (b > 0).astype(F32)
    has_north = (b < lat_n - 1).astype(F32)
    cols = [slice(i * band, (i + 1) * band) for i in range(slab)]

    def copies(par, h):
        span = pl.ds(h * rows_h, min(rows_h, valid - (h % per_var) * rows_h))
        return [
            pltpu.make_async_remote_copy(
                src_ref=snd.at[par, d, span],
                dst_ref=rcv.at[par, d, span],
                send_sem=ssem.at[par, h, d],
                recv_sem=rsem.at[par, h, d],
                device_id=peers[d],
                device_id_type=MESH,
            )
            for d in range(4)
        ]

    def start(par, h):
        for copy in copies(par, h):
            copy.start()

    def wait(par, h):
        for copy in copies(par, h):
            copy.wait()

    def tiles(h, body, carry=None):
        for n in range(rows_h // TILE):
            row = pl.ds(h * rows_h + n * TILE, TILE)
            crow = pl.ds((h % per_var) * rows_h + n * TILE, TILE)
            carry = body(row, crow, carry)
        return carry

    def winds(t, crow):
        return (
            [courant[t, 0, i, crow, :] for i in range(slab)],
            [courant[t, 1, i, crow, :] for i in range(slab)],
        )

    def load(ref, row):
        return [ref[row, c] for c in cols]

    def store(ref, row, values):
        for c, value in zip(cols, values):
            ref[row, c] = value

    def turn(value, shift):
        shift = shift % band
        return value if shift == 0 else pltpu.roll(value, shift, 1)

    def halos(par, row):
        from_south = rcv[par, 3, row, :] * has_south
        from_north = rcv[par, 2, row, :] * has_north
        return rcv[par, 1, row, :], rcv[par, 0, row, :], from_south, from_north

    def shifted(value, halo, i, up):
        if up:
            return jnp.where(lane == 0, turn(halo, -i), turn(value, 1))
        return jnp.where(lane == band - 1, turn(halo, slab - 1 - i), turn(value, -1))

    def advance(t, row, crow, par):
        u, v = winds(t, crow)
        x = load(s, row)
        west, east, south, north = halos(par, row)
        full = [west] + x + [east]
        outs = []
        for i in range(slab):
            out = (1.0 - jnp.abs(u[i]) - jnp.abs(v[i])) * x[i]
            out += jnp.maximum(u[i], 0.0) * full[i]
            out += jnp.maximum(-u[i], 0.0) * full[i + 2]
            out += jnp.maximum(v[i], 0.0) * shifted(x[i], south, i, True)
            out += jnp.maximum(-v[i], 0.0) * shifted(x[i], north, i, False)
            outs.append(out)
        return outs

    def retreat(t, row, crow, par):
        u, v = winds(t, crow)
        y = load(s, row)
        west, east, south, north = halos(par, row)
        plus = [jnp.maximum(u[i], 0.0) * y[i] for i in range(slab)] + [east]
        minus = [west] + [jnp.maximum(-u[i], 0.0) * y[i] for i in range(slab)]
        outs = []
        for i in range(slab):
            out = (1.0 - jnp.abs(u[i]) - jnp.abs(v[i])) * y[i]
            out += plus[i + 1] + minus[i]
            out += shifted(jnp.maximum(v[i], 0.0) * y[i], north, i, False)
            out += shifted(jnp.maximum(-v[i], 0.0) * y[i], south, i, True)
            outs.append(out)
        return outs

    def put_edges(par, row, west, east, southward, northward):
        snd[par, 0, row, :] = west
        snd[par, 1, row, :] = east
        low = jnp.zeros((TILE, band), F32)
        high = low
        for i in range(slab):
            low = jnp.where(lane == band - slab + i, turn(southward[i], band - slab + i), low)
            high = jnp.where(lane == i, turn(northward[i], i + 1), high)
        snd[par, 2, row, :] = low
        snd[par, 3, row, :] = high

    def put_state(par, row, x):
        put_edges(par, row, x[0], x[-1], x, x)

    def put_products(par, t, row, crow, y):
        u, v = winds(t, crow)
        put_edges(
            par, row,
            jnp.maximum(u[0], 0.0) * y[0],
            jnp.maximum(-u[-1], 0.0) * y[-1],
            [jnp.maximum(v[i], 0.0) * y[i] for i in range(slab)],
            [jnp.maximum(-v[i], 0.0) * y[i] for i in range(slab)],
        )

    def project(var):
        high, low = split(s[var * levels : (var + 1) * levels, :])
        y = dot(up_w[var], jnp.concatenate([high, high, low], axis=0))
        if var == 0:
            y_acc[...] = y
        else:
            y_acc[...] += y

    def scatter(t, weighted):
        pair = jnp.concatenate(split(weighted), axis=0)
        both = dot_nt(pair, onehot[t])
        high, low = split(both[:chan] + both[chan:])
        v_dep[t, :chan, :] = high
        v_dep[t, chan : 2 * chan, :] = high
        v_dep[t, 2 * chan :, :] = low

    def observe(t):
        pair = jnp.concatenate(split(y_acc[...]), axis=0)
        both = dot(pair, onehot[t])
        scatter(t, scale[t] * (both[:chan] + both[chan:]))

    def deposit(t, var, into):
        span = slice(var * levels, (var + 1) * levels)
        into[span, :] = dot(down_w[span, :], v_dep[t])

    def adjoint(finish, carry, pass_on):
        for var in range(2):
            deposit(times - 1, var, s)
            for h in range(var * per_var, (var + 1) * per_var):
                def enter(row, crow, none):
                    put_products(0, times - 1, row, crow, load(s, row))

                tiles(h, enter)
                start(0, h)

        def step(n, none):
            t = times - 1 - n
            par = lax.rem(n, 2)
            for var in range(2):
                deposit(t - 1, var, dep)
            for h in range(CHUNKS):
                wait(par, h)

                def back(row, crow, none):
                    y = [v + d for v, d in zip(retreat(t, row, crow, par), load(dep, row))]
                    store(s, row, y)
                    put_products(1 - par, t - 1, row, crow, y)

                tiles(h, back)
                start(1 - par, h)
            return none

        lax.fori_loop(0, times - 1, step, 0)
        par = (times - 1) % 2
        for h in range(CHUNKS):
            wait(par, h)

            def last(row, crow, carry):
                return finish(row, retreat(0, row, crow, par), carry)

            carry = tiles(h, last, carry)
            if pass_on:
                start(0, h)
        return carry

    def tangent(k):
        def step(t, none):
            par = lax.rem(t, 2)
            for h in range(CHUNKS):
                if k == 0:
                    wait(par, h)
                    span = slice(h * rows_h, (h + 1) * rows_h)

                    @pl.when(t == 0)
                    def _():
                        keep[:, span, :] = rcv[0, :, span, :]
                else:

                    @pl.when(t == 0)
                    def _():
                        blends[-1](h)

                    @pl.when(t > 0)
                    def _():
                        wait(par, h)

                def onward(row, crow, none):
                    x = advance(t, row, crow, par)
                    store(s, row, x)
                    put_state(1 - par, row, x)

                tiles(h, onward)
                start(1 - par, h)
                if (h + 1) % per_var == 0:
                    project(h // per_var)
            observe(t)
            return none

        lax.fori_loop(0, times - 1, step, 0)
        par = (times - 1) % 2
        for h in range(CHUNKS):
            wait(par, h)

            def last(row, crow, none):
                store(s, row, advance(times - 1, row, crow, par))

            tiles(h, last)
            if (h + 1) % per_var == 0:
                project(h // per_var)
        observe(times - 1)

    def across(k, axis, tile, count, me, source, sums, send, receive):
        source[k] = tile
        sums[k, me] = tile
        moves = []
        for off in range(1, count):
            other = lax.rem(me + off, count)
            moves.append(
                pltpu.make_async_remote_copy(
                    src_ref=source.at[k],
                    dst_ref=sums.at[k, me],
                    send_sem=send.at[k, off - 1],
                    recv_sem=receive.at[k, off - 1],
                    device_id=(other, b) if axis == 0 else (a, other),
                    device_id_type=MESH,
                )
            )
        for move in moves:
            move.start()
        for move in moves:
            move.wait()
        total = sums[k, 0]
        for j in range(1, count):
            total = total + sums[k, j]
        return total

    def allsum(k, first, second, third):
        tile = jnp.concatenate([first, second, third], axis=0)
        tile = across(k, 0, tile, lon_n, a, part1, sums1, s1, r1)
        tile = across(k, 1, tile, lat_n, b, part2, sums2, s2, r2)
        return [jnp.sum(tile[8 * n : 8 * n + 8], keepdims=True) for n in range(3)]

    def fold(value):
        return value.reshape(TILE // 8, 8, band).sum(0)

    slots = cells.shape[-1]
    place = lax.broadcasted_iota(jnp.int32, (slab * band, slots), 0)
    for t in range(times):
        here = jnp.broadcast_to(cells[t], (slab * band, slots))
        onehot[t] = jnp.where(here == place, 1.0, 0.0).astype(BF16)
        scatter(t, target[t])
    pl.semaphore_wait(barrier, lon_n + lat_n - 2)

    zero = jnp.zeros((8, band), F32)

    def begin(row, values, acc):
        put_state(0, row, values)
        for value in values:
            acc = acc + fold(value * value)
        store(s, row, values)
        store(p, row, values)
        store(r_out, row, values)
        return acc

    def imager(pass_on):
        def image(row, values, carry):
            pq, qq = carry
            outs = []
            for d, value in zip(load(p, row), values):
                q = d + value
                outs.append(q)
                pq = pq + fold(d * q)
                qq = qq + fold(q * q)
            store(s, row, outs)
            if pass_on:
                put_state(0, row, outs)
            return pq, qq

        return image

    acc = adjoint(begin, zero, True)
    rho = None
    blends = []
    for k in range(ITERS):
        last = k + 1 == ITERS
        tangent(k)
        pq, qq = adjoint(imager(not last), (zero, zero), not last)
        pq, qq, rr = allsum(k, pq, qq, acc)
        if k == 0:
            rho = rr
        alpha = rho / pq
        if not last:
            rho_new = rho - 2.0 * alpha * pq + alpha * alpha * qq
            beta = rho_new / rho
            rho = rho_new
        for h in range(CHUNKS):
            def update(row, crow, none):
                d = load(p, row)
                q = load(s, row)
                old_r = load(r_out, row)
                step = [alpha * v for v in d]
                if k > 0:
                    step = [v + w for v, w in zip(step, load(x_out, row))]
                store(x_out, row, step)
                residual = [v - alpha * w for v, w in zip(old_r, q)]
                store(r_out, row, residual)
                if not last:
                    d = [v + beta * w for v, w in zip(residual, d)]
                    store(p, row, d)
                    store(s, row, d)

            tiles(h, update)
        if not last:
            def mixed(h, alpha=alpha, beta=beta):
                wait(0, h)

                def mix(row, crow, none):
                    for d in range(4):
                        old = keep[d, row, :]
                        rcv[0, d, row, :] = (old - alpha * rcv[0, d, row, :]) + beta * old

                tiles(h, mix)

            blends.append(mixed)


def pair_of(value):
    high = lax.reduce_precision(value, 8, 7)
    return high, lax.reduce_precision(value - high, 8, 7)


def body(courant, slot_column_cells, column_counts, innovations, error_weight, weighting):
    times, _, levels, slab, band = courant.shape
    owners, cap = slot_column_cells.shape[2:]
    chan = weighting.shape[1]
    slots = owners * cap
    lon_n, lat_n = lax.axis_size("lon"), lax.axis_size("lat")
    deep = -(-levels // 48) * 48

    field = jnp.pad(courant.transpose(0, 1, 3, 2, 4), ((0, 0),) * 3 + ((0, deep - levels), (0, 0)))
    weights = jnp.pad(weighting.reshape(2, levels, chan), ((0, 0), (0, deep - levels), (0, 0)))
    high, low = pair_of(weights)
    down_w = jnp.concatenate([high, low, high], axis=2).reshape(2 * deep, 3 * chan).astype(BF16)
    up_w = jnp.concatenate([high, low, high], axis=1).transpose(0, 2, 1).astype(BF16)
    here = error_weight[:, 0]
    both = jnp.stack([here, here * innovations[:, 0]]).transpose(2, 0, 1, 3, 4)
    both = lax.all_to_all(both, ("lon", "lat"), split_axis=0, concat_axis=0, tiled=True)
    position = lax.broadcasted_iota(jnp.int32, (times, owners, cap), 2)
    live = (position < column_counts[:, 0][:, :, None]).astype(F32).reshape(times, 1, slots)
    both = both.transpose(1, 2, 4, 0, 3).reshape(2, times, chan, slots) * live
    cells = slot_column_cells[:, 0].reshape(times, 1, slots)

    state = (2 * deep, slab * band)
    vmem = pl.BlockSpec(memory_space=pltpu.VMEM)
    sums = ITERS
    x, r = pl.pallas_call(
        functools.partial(kernel, lon_n, lat_n, levels),
        out_shape=[jax.ShapeDtypeStruct(state, F32)] * 2,
        in_specs=[vmem] * 6,
        out_specs=[vmem] * 2,
        scratch_shapes=[
            pltpu.VMEM(state, F32),
            pltpu.VMEM(state, F32),
            pltpu.VMEM((4, 2 * deep, band), F32),
            pltpu.VMEM(state, F32),
            pltpu.VMEM((chan, slab * band), F32),
            pltpu.VMEM((times, 3 * chan, slab * band), BF16),
            pltpu.VMEM((times, slab * band, slots), BF16),
            pltpu.VMEM((2, 4, 2 * deep, band), F32),
            pltpu.VMEM((2, 4, 2 * deep, band), F32),
            pltpu.VMEM((sums, 24, band), F32),
            pltpu.VMEM((sums, 24, band), F32),
            pltpu.VMEM((sums, lon_n, 24, band), F32),
            pltpu.VMEM((sums, lat_n, 24, band), F32),
            pltpu.SemaphoreType.DMA((2, CHUNKS, 4)),
            pltpu.SemaphoreType.DMA((2, CHUNKS, 4)),
            pltpu.SemaphoreType.DMA((sums, lon_n - 1)),
            pltpu.SemaphoreType.DMA((sums, lon_n - 1)),
            pltpu.SemaphoreType.DMA((sums, lat_n - 1)),
            pltpu.SemaphoreType.DMA((sums, lat_n - 1)),
        ],
        compiler_params=pltpu.CompilerParams(collective_id=0, has_side_effects=True, vmem_limit_bytes=48 * 2**20),
    )(field, cells, both[0], both[1], up_w, down_w)

    def back(state):
        return state.reshape(2, deep, slab, band)[:, :levels]

    return back(x), back(r)


def solution(mesh):
    owned = ("lon", "lat")
    in_specs = (
        P(None, None, None, "lon", "lat"),
        P(None, owned, None, None),
        P(None, owned, None),
        P(None, owned, None, None, None),
        P(None, owned, None, None, None),
        P(),
    )
    out_specs = (P(None, None, "lon", "lat"), P(None, None, "lon", "lat"))
    return jax.shard_map(body, mesh=mesh, in_specs=in_specs, out_specs=out_specs, check_vma=False)
```
